32 devices in a mesh: mp: 2 (over y), fsdp: 8 (over z, core), tp: 2 (over x).
Axes of the slice: x: 2, y: 2, z: 4, core: 2. Of those that a mesh axis runs over, the one named last changes fastest.
Arguments:
- hidden: bfloat16 [2, 1280, 5120], P('mp', 'fsdp'), may hold values from -6 to 6
- live_weight: bfloat16 [2, 5120, 1024], P('mp', 'fsdp', 'tp'), may hold values from -0.078125 to 0.078125
- stale_weight: bfloat16 [2, 5120, 1024], P('mp', 'fsdp', 'tp'), may hold values from -0.078125 to 0.078125
- match: int32 [2, 1280], P('mp', 'fsdp'), may hold values from 0 to 159, as said below
Outputs:
- hidden_grad: bfloat16 [2, 1280, 5120], P('mp', 'fsdp', 'tp')
The draws below stay inside these ranges and needn't reach their ends.
Inputs may be any that keep to these rules, and one draw needn't show every extreme that they name: Within each model's block of 160 rows, match is a permutation of 0 to 159, and the two models' permutations of a block are inverse to each other.
All inputs are finite; a program needn't handle non-finite values.
Results may differ from the reference program's by a relative error of at most 0.0061.
Values may be sent and summed in bfloat16 or wider, within the bound.
No kernel may reach another device: no remote copies, remote signals or barrier semaphores. Data moves between devices by JAX's collectives and lax.ppermute only.
A program may use at most 64 MiB of HBM per device.

```python
import jax
import jax.numpy as jnp
from jax import lax

D = 5120
KVW = 1024
TOK_DEV = 160
TOKENS = 1280
N_TP = 2


def draw_match(key, part):
    count = TOKENS // TOK_DEV
    subkeys = jax.random.split(key, count)

    def one_order(subkey):
        return jax.random.permutation(subkey, TOK_DEV)
    orders = jax.vmap(one_order)(subkeys).astype(jnp.int32)
    inverse = jnp.argsort(orders, axis=1, stable=True).astype(jnp.int32)
    return jnp.stack([orders, inverse]).reshape(2, TOKENS).astype(jnp.int32)


def shard_levels(own_key, dims, cuts, low, largest):
    loudness, own = 1.0, jax.random.fold_in(own_key, 6)
    for position, blocks in cuts:
        draws = jnp.exp(jax.random.uniform(jax.random.fold_in(own, position), (blocks,), jnp.float32, low / len(cuts), largest / len(cuts)))
        loudness = loudness * jnp.repeat(draws, dims[position] // blocks).reshape([-1 if axis == position else 1 for axis in range(len(dims))])
    return loudness


def noise(stream_key, shape, scale, reach, shards=(), held_as=jnp.bfloat16):
    result = jax.random.normal(stream_key, shape, jnp.float32) * scale
    if len(shards) > 0:
        result = shard_levels(stream_key, shape, shards, -0.22, 0.18) * result
    return jnp.clip(result, min=-reach, max=reach).astype(held_as)


def setup_inputs(seed: int = 0) -> dict:
    seeds = jax.random.split(jax.random.key(seed), 5)
    return {
        "hidden": noise(seeds[0], (2, TOKENS, D), 1.0, 6.0, ((0, 2), (1, 8))),
        "live_weight": noise(seeds[1], (2, D, KVW), D ** -0.5, 0.078125, ((0, 2), (1, 8), (2, 2))),
        "stale_weight": noise(seeds[2], (2, D, KVW), D ** -0.5, 0.078125, ((0, 2), (1, 8), (2, 2))),
        "match": draw_match(jax.random.fold_in(seeds[4], 71), 0),
    }


def reference(hidden, live_weight, stale_weight, match):
    blocks = TOKENS // TOK_DEV
    width = KVW // N_TP
    results = []
    for model in range(2):
        other = 1 - model
        student = jnp.dot(hidden[model], live_weight[model], preferred_element_type=jnp.float32)
        teacher = jnp.dot(hidden[other], stale_weight[other], preferred_element_type=jnp.float32).astype(jnp.bfloat16)
        teacher = lax.optimization_barrier(teacher)
        grouped = teacher.reshape(blocks, TOK_DEV, KVW)
        lookup = match[model].reshape(blocks, TOK_DEV).astype(jnp.int32)
        target = jnp.take_along_axis(grouped, lookup[:, :, None], axis=1).reshape(TOKENS, KVW)
        mismatch = (student - target.astype(jnp.float32)).astype(jnp.bfloat16)
        running = jnp.zeros((TOKENS, D), jnp.float32)
        for group in range(N_TP):
            left = mismatch[:, group * width:(group + 1) * width]
            right = live_weight[model][:, group * width:(group + 1) * width]
            partial_value = jnp.dot(left, right.T, preferred_element_type=jnp.float32).astype(jnp.bfloat16)
            partial_value = lax.optimization_barrier(partial_value)
            running = running + partial_value.astype(jnp.float32)
        results.append(running.astype(jnp.bfloat16))
    return jnp.stack(results)
```

```python
import jax
import jax.numpy as jnp
from jax import lax
from jax.sharding import PartitionSpec as P

PAIR = ((0, 1), (1, 0), (2, 3), (3, 2))
MID = ((1, 2), (2, 1))
OUT = ((1, 0), (2, 3))
IN = ((0, 1), (3, 2))


def partner(block, axis, apart):
    count = lax.axis_size(axis)
    route = []
    for low in range(count):
        high = low | 1 << apart
        if high != low and high < count:
            route += [(low, high), (high, low)]
    return lax.ppermute(block, axis, route)


def along_z(block, pairs):
    route = [(2 * a + c, 2 * b + c) for a, b in pairs for c in range(2)]
    return lax.ppermute(block, "fsdp", route)


def across_cores(block):
    return partner(block, "fsdp", 0)


def near_over_x(block, near):
    route = []
    for f in range(8):
        own = f // 4
        source = 1 - own if near else own
        route.append((2 * f + source, 2 * f + 1 - source))
    return lax.ppermute(block, ("fsdp", "tp"), route)


def after(values, *gates):
    out = lax.optimization_barrier((tuple(values), gates))
    return out[0]


def dot(a, b):
    return jnp.dot(a, b, preferred_element_type=jnp.float32)


def dot_t(a, b):
    return lax.dot_general(a, b, (((1,), (1,)), ((), ())), preferred_element_type=jnp.float32)


def general(hidden, live_weight, stale_weight, match):
    hidden_rows = hidden[0]
    live_full = lax.all_gather(live_weight[0], "fsdp", axis=0, tiled=True)
    student = dot(hidden_rows, live_full)
    stale_full = lax.all_gather(stale_weight[0], "fsdp", axis=0, tiled=True)
    teacher = dot(hidden_rows, stale_full).astype(jnp.bfloat16)
    teacher = partner(teacher, "mp", 0)
    target = jnp.take(teacher, match[0], axis=0)
    mismatch = (student - target.astype(jnp.float32)).astype(jnp.bfloat16)
    partial_value = dot_t(mismatch, live_full).astype(jnp.bfloat16)
    summed = lax.psum_scatter(partial_value, "tp", scatter_dimension=1, tiled=True)
    return summed[None]


def line_of_four(hidden, live_weight, stale_weight, match):
    h, live, stale = hidden[0], live_weight[0], stale_weight[0]
    tokens, width = h.shape
    rows, cols = live.shape
    f, x = lax.axis_index("fsdp"), lax.axis_index("tp")
    z, c = f // 2, f % 2
    half = z // 2
    end = (z == 0) | (z == 3)
    q_opp = jnp.where(half == 0, 2, 1)
    q_far = jnp.where(half == 0, 3, 0)

    def h_rows(base, q):
        mine = lax.dynamic_slice_in_dim(base, rows * (2 * q + c), rows, 1)
        other = lax.dynamic_slice_in_dim(base, rows * (2 * q + 1 - c), rows, 1)
        return mine, other

    def contrib(base, q, piece, piece_other):
        mine, other = h_rows(base, q)
        return dot(mine, piece) + dot(other, piece_other)

    far_half = lax.dynamic_slice_in_dim(h, (width // 2) * (1 - half), width // 2, 1)

    live_nb = along_z(live, PAIR)
    live_opp_mid = along_z(live, MID)
    live_o = across_cores(live)
    stale_o = across_cores(stale)
    x_own = near_over_x(live, True)

    live_far_mid = along_z(live_nb, MID)
    live_opp_end = along_z(live_opp_mid, OUT)
    stale_1, far_half = after((stale, far_half), live_nb, live_opp_mid)
    stale_nb = along_z(stale_1, PAIR)
    stale_opp = along_z(stale_1, MID)
    h_end = along_z(far_half, IN)
    x_nb = near_over_x(live_nb, True)
    live_nb_o = across_cores(live_nb)
    live_opp = jnp.where(end, live_opp_end, live_opp_mid)
    live_opp_o = across_cores(live_opp)
    x_opp = near_over_x(live_opp, False)

    live_far_end = along_z(live_far_mid, OUT)
    (stale_nb_2,) = after((stale_nb,), live_far_mid)
    stale_far = along_z(stale_nb_2, MID)
    stale_nb_o = across_cores(stale_nb)
    stale_opp_o = across_cores(stale_opp)
    live_far = jnp.where(end, live_far_end, live_far_mid)
    live_far_o = across_cores(live_far)
    x_far = near_over_x(live_far, False)

    student = (
        contrib(h, z, live, live_o)
        + contrib(h, z ^ 1, live_nb, live_nb_o)
        + contrib(h, q_opp, live_opp, live_opp_o)
        + contrib(h, q_far, live_far, live_far_o)
    )

    t_own = contrib(h, z, stale, stale_o) + contrib(h, z ^ 1, stale_nb, stale_nb_o)
    own_far = lax.dynamic_slice_in_dim(h, (width // 2) * (1 - half), width // 2, 1)
    both = jnp.concatenate([own_far, h_end], axis=0)
    base = 2 * (1 - half)
    t_other = contrib(both, q_opp - base, stale_opp, stale_opp_o)
    stale_far_o = across_cores(stale_far)
    t_other = t_other + contrib(both, q_far - base, stale_far, stale_far_o)
    t_mine = t_own + jnp.where(end, 0.0, t_other[:tokens])
    t_mine = t_mine.astype(jnp.bfloat16)
    t_end = t_other[tokens:].astype(jnp.bfloat16)

    target_1 = partner(t_mine, "mp", 0)
    route = []
    for m in range(2):
        for a, b in OUT:
            for core in range(2):
                route.append((8 * m + 2 * a + core, 8 * (1 - m) + 2 * b + core))
    target_2 = lax.ppermute(t_end, ("mp", "fsdp"), route)
    teacher = (target_1.astype(jnp.float32) + target_2.astype(jnp.float32)).astype(jnp.bfloat16)
    pick = (match[0][:, None] == lax.broadcasted_iota(jnp.int32, (tokens, tokens), 1)).astype(jnp.bfloat16)
    target = dot(pick, teacher)
    mismatch = (student - target).astype(jnp.bfloat16)
    mismatch_o = partner(mismatch, "tp", 0)

    near = half == x
    a_own = jnp.where(near, live, live_opp)
    a_own_o = jnp.where(near, live_o, live_opp_o)
    b_own = jnp.where(near, live_nb, live_far)
    b_own_o = jnp.where(near, live_nb_o, live_far_o)
    a_x = jnp.where(near, x_own, x_opp)
    b_x = jnp.where(near, x_nb, x_far)
    a_x_o = across_cores(a_x)
    b_x_o = across_cores(b_x)
    place_a = jnp.where(near, z % 2, half)
    place_b = 1 - place_a

    def ordered(pa, pao, pb, pbo):
        full = jnp.zeros((4 * rows, cols), jnp.bfloat16)
        full = lax.dynamic_update_slice_in_dim(full, pa, rows * (2 * place_a + c), 0)
        full = lax.dynamic_update_slice_in_dim(full, pao, rows * (2 * place_a + 1 - c), 0)
        full = lax.dynamic_update_slice_in_dim(full, pb, rows * (2 * place_b + c), 0)
        full = lax.dynamic_update_slice_in_dim(full, pbo, rows * (2 * place_b + 1 - c), 0)
        return full

    w_own = ordered(a_own, a_own_o, b_own, b_own_o)
    w_x = ordered(a_x, a_x_o, b_x, b_x_o)
    grad = dot_t(mismatch, w_own) + dot_t(mismatch_o, w_x)
    return grad.astype(jnp.bfloat16)[None]


def solution(mesh):
    in_specs = (
        P("mp", "fsdp", None),
        P("mp", "fsdp", "tp"),
        P("mp", "fsdp", "tp"),
        P("mp", "fsdp"),
    )
    out_specs = P("mp", "fsdp", "tp")
    line = mesh.shape["fsdp"] == 8 and mesh.shape["tp"] == 2 and mesh.shape["mp"] == 2
    body = line_of_four if line else general
    return jax.shard_map(body, mesh=mesh, in_specs=in_specs, out_specs=out_specs, check_vma=False)
```

```python
import jax
import jax.numpy as jnp
import numpy as np
from jax import lax
from jax.experimental import pallas as pl
from jax.experimental.pallas import tpu as pltpu
from jax.sharding import PartitionSpec as P

PAIR = ((0, 1), (1, 0), (2, 3), (3, 2))
MID = ((1, 2), (2, 1))
OUT = ((1, 0), (2, 3))

OWN, OWN_O, NB, NB_O, OPP, OPP_O, FAR, FAR_O, END, NEAR, HALF, PIECE = range(12)


def table():
    rows = []
    for f in range(8):
        for x in range(2):
            z, c = f // 2, f % 2
            half = z // 2
            opp, far = (2, 3) if half == 0 else (1, 0)
            near = int(half == x)
            first = z % 2 if near else half
            row = []
            for q in (z, z ^ 1, opp, far):
                row += [2 * q + c, 2 * q + 1 - c]
            row += [int(z in (0, 3)), near, 1 - half]
            for q in (first, 1 - first):
                row += [2 * q + c, 2 * q + 1 - c]
            rows.append(row)
    return np.array(rows, np.int32)


def partner(block, axis, apart):
    count = lax.axis_size(axis)
    route = []
    for low in range(count):
        high = low | 1 << apart
        if high != low and high < count:
            route += [(low, high), (high, low)]
    return lax.ppermute(block, axis, route)


def along_z(block, pairs):
    route = [(2 * a + c, 2 * b + c) for a, b in pairs for c in range(2)]
    return lax.ppermute(block, "fsdp", route)


def across_cores(block):
    return partner(block, "fsdp", 0)


def near_over_x(block, near):
    route = []
    for f in range(8):
        own = f // 4
        source = 1 - own if near else own
        route.append((2 * f + source, 2 * f + 1 - source))
    return lax.ppermute(block, ("fsdp", "tp"), route)


def after(values, *gates):
    out = lax.optimization_barrier((tuple(values), gates))
    return out[0]


def dot(a, b):
    return jnp.dot(a, b, preferred_element_type=jnp.float32)


def dot_t(a, b):
    return lax.dot_general(a, b, (((1,), (1,)), ((), ())), preferred_element_type=jnp.float32)


def whole(array):
    return pl.BlockSpec(array.shape, lambda i, s: (0,) * array.ndim)


def call(body, places, operands, specs, outs, scratch=(), name=None):
    single = not isinstance(outs, (list, tuple))
    shapes = [outs] if single else list(outs)
    out = pl.pallas_call(
        body,
        out_shape=shapes,
        grid_spec=pltpu.PrefetchScalarGridSpec(
            num_scalar_prefetch=1,
            grid=(1,),
            in_specs=specs,
            out_specs=[pl.BlockSpec(o.shape, lambda i, s, n=len(o.shape): (0,) * n) for o in shapes],
            scratch_shapes=list(scratch),
        ),
        cost_estimate=pl.CostEstimate(flops=1, bytes_accessed=1, transcendentals=0),
        name=name,
    )(places, *operands)
    return out[0] if single else out


ANY = pl.BlockSpec(memory_space=pl.ANY)


def contrib(places, h, mine, other, weight, weight_o, total=None):
    tokens, rows, cols = h.shape[0], *weight.shape

    def body(s, *refs):
        if total is None:
            a, b, w, wo, out = refs
            out[...] = dot(a[...], w[...]) + dot(b[...], wo[...])
        else:
            t, a, b, w, wo, out = refs
            out[...] = t[...] + dot(a[...], w[...]) + dot(b[...], wo[...])

    specs = [
        pl.BlockSpec((tokens, rows), lambda i, s: (0, s[mine])),
        pl.BlockSpec((tokens, rows), lambda i, s: (0, s[other])),
        whole(weight),
        whole(weight_o),
    ]
    operands = [h, h, weight, weight_o]
    if total is not None:
        specs.insert(0, whole(total))
        operands.insert(0, total)
    return call(body, places, operands, specs, jax.ShapeDtypeStruct((tokens, cols), jnp.float32), name="contrib")


def send_or_pass(places, h, piece, first, count):
    tokens, (rows, cols) = h.shape[0], piece.shape
    per_half = h.shape[1] // 2 // cols

    def body(s, *refs):
        blocks, piece_ref, out, sem = refs[:count], refs[count], refs[count + 1], refs[count + 2]

        @pl.when(s[END] == 1)
        def _():
            for k in range(count):
                out[k * tokens:(k + 1) * tokens, :] = blocks[k][...]
            if count * tokens < rows:
                out[count * tokens:, :] = jnp.zeros((rows - count * tokens, cols), out.dtype)

        @pl.when(s[END] == 0)
        def _():
            copy = pltpu.make_async_copy(piece_ref, out, sem)
            copy.start()
            copy.wait()

    specs = [
        pl.BlockSpec((tokens, cols), lambda i, s, k=k: (0, s[HALF] * per_half + first + k))
        for k in range(count)
    ]
    return call(
        body, places, [h] * count + [piece], specs + [ANY],
        jax.ShapeDtypeStruct(piece.shape, piece.dtype), [pltpu.SemaphoreType.DMA], name="send_or_pass",
    )


def choose(places, flag, yes, no):
    def body(s, yes_ref, no_ref, out, sem):
        @pl.when(s[flag] == 1)
        def _():
            copy = pltpu.make_async_copy(yes_ref, out, sem)
            copy.start()
            copy.wait()

        @pl.when(s[flag] == 0)
        def _():
            copy = pltpu.make_async_copy(no_ref, out, sem)
            copy.start()
            copy.wait()

    return call(
        body, places, [yes, no], [ANY, ANY], jax.ShapeDtypeStruct(yes.shape, yes.dtype),
        [pltpu.SemaphoreType.DMA], name="choose",
    )


def teachers(places, h, t_near, stale_opp, stale_opp_o, stale_far, stale_far_o, came_a, came_b):
    tokens, (rows, cols) = h.shape[0], stale_opp.shape
    fit = rows // tokens
    width = h.shape[1] // 2

    def body(s, near, p, po, r, ro, w, wo, v, vo, ca, cb, mine, sent, held):
        for k in range(width // cols):
            source = ca if k < fit else cb
            j = k if k < fit else k - fit
            held[:, k * cols:(k + 1) * cols] = source[j * tokens:(j + 1) * tokens, :]

        def cut(place):
            start = (s[place] - s[HALF] * (width // rows)) * rows
            return held[:, pl.ds(pl.multiple_of(start, 128), rows)]

        far = dot(p[...], w[...]) + dot(po[...], wo[...]) + dot(r[...], v[...]) + dot(ro[...], vo[...])
        mine[...] = (near[...] + jnp.where(s[END] == 1, 0.0, far)).astype(mine.dtype)
        end = dot(cut(OPP), w[...]) + dot(cut(OPP_O), wo[...])
        end = end + dot(cut(FAR), v[...]) + dot(cut(FAR_O), vo[...])
        sent[...] = end.astype(sent.dtype)

    def block(place):
        return pl.BlockSpec((tokens, rows), lambda i, s: (0, s[place]))

    operands = [t_near, h, h, h, h, stale_opp, stale_opp_o, stale_far, stale_far_o, came_a, came_b]
    specs = [whole(t_near), block(OPP), block(OPP_O), block(FAR), block(FAR_O)]
    specs += [whole(o) for o in operands[5:]]
    out = jax.ShapeDtypeStruct((tokens, cols), jnp.bfloat16)
    return call(
        body, places, operands, specs, [out, out], [pltpu.VMEM((tokens, width), h.dtype)], name="teachers"
    )


def difference(places, student, target_1, target_2, match):
    tokens = student.shape[0]

    def body(s, student_ref, one, two, match_ref, out):
        teacher = (one[...].astype(jnp.float32) + two[...].astype(jnp.float32)).astype(jnp.bfloat16)
        rows = lax.broadcasted_iota(jnp.int32, (tokens, tokens), 0)
        pick = (match_ref[...] == rows).astype(jnp.bfloat16)
        target = lax.dot_general(
            pick, teacher, (((0,), (0,)), ((), ())), preferred_element_type=jnp.float32
        )
        out[...] = (student_ref[...] - target).astype(out.dtype)

    operands = [student, target_1, target_2, match]
    return call(
        body, places, operands, [whole(o) for o in operands],
        jax.ShapeDtypeStruct(student.shape, jnp.bfloat16), name="difference",
    )


def gradient(places, left, left_o, near_own, far_own, near_x, far_x):
    tokens = left.shape[0]
    rows, cols = near_own[0].shape

    def body(s, left_ref, left_o_ref, *refs):
        sources, out, held, sems = refs[:16], refs[16], refs[17], refs[18]

        def copies(near):
            picked = []
            for k in range(4):
                picked.append(sources[k if near else 4 + k])
                picked.append(sources[8 + k if near else 12 + k])
            return [
                pltpu.make_async_copy(picked[j], held.at[j], sems.at[j]) for j in range(8)
            ]

        for near in (0, 1):
            @pl.when(s[NEAR] == near)
            def _(near=near):
                started = copies(near)
                for copy in started:
                    copy.start()
                for copy in started:
                    copy.wait()
        for k in range(4):
            value = dot_t(left_ref[...], held[2 * k]) + dot_t(left_o_ref[...], held[2 * k + 1])
            start = pl.multiple_of(s[PIECE + k] * rows, 128)
            out[:, pl.ds(start, rows)] = value.astype(out.dtype)

    operands = [left, left_o, *near_own, *far_own, *near_x, *far_x]
    return call(
        body, places, operands, [whole(left), whole(left_o)] + [ANY] * 16,
        jax.ShapeDtypeStruct((tokens, 4 * rows), jnp.bfloat16),
        [pltpu.VMEM((8, rows, cols), left.dtype), pltpu.SemaphoreType.DMA((8,))], name="gradient",
    )


def general(hidden, live_weight, stale_weight, match):
    hidden_rows = hidden[0]
    live_full = lax.all_gather(live_weight[0], "fsdp", axis=0, tiled=True)
    student = dot(hidden_rows, live_full)
    stale_full = lax.all_gather(stale_weight[0], "fsdp", axis=0, tiled=True)
    teacher = dot(hidden_rows, stale_full).astype(jnp.bfloat16)
    teacher = partner(teacher, "mp", 0)
    target = jnp.take(teacher, match[0], axis=0)
    mismatch = (student - target.astype(jnp.float32)).astype(jnp.bfloat16)
    partial_value = dot_t(mismatch, live_full).astype(jnp.bfloat16)
    summed = lax.psum_scatter(partial_value, "tp", scatter_dimension=1, tiled=True)
    return summed[None]


def line_of_four(hidden, live_weight, stale_weight, match):
    h, live, stale = hidden[0], live_weight[0], stale_weight[0]
    fit = live.shape[0] // h.shape[0]
    place = 2 * lax.axis_index("fsdp") + lax.axis_index("tp")
    places = lax.dynamic_index_in_dim(jnp.asarray(table()), place, 0, keepdims=False)

    live_mid = along_z(live, MID)
    live_nb = along_z(live, PAIR)
    stale_opp = along_z(stale, MID)
    stale_nb = along_z(stale, PAIR)
    x_own = near_over_x(live, True)
    live_o = across_cores(live)
    stale_o = across_cores(stale)
    student = contrib(places, h, OWN, OWN_O, live, live_o)
    t_near = contrib(places, h, OWN, OWN_O, stale, stale_o)

    mid_2, nb_2 = after((live_mid, live_nb), stale_opp, stale_nb, student, t_near)
    live_far_mid = along_z(nb_2, MID)
    came_a = along_z(send_or_pass(places, h, mid_2, 0, fit), PAIR)
    nb_x, stale_nb_2, stale_opp_2 = after((nb_2, stale_nb, stale_opp), x_own, live_o, stale_o)
    x_nb = near_over_x(nb_x, True)
    live_nb_o = across_cores(nb_x)
    stale_nb_o = across_cores(stale_nb_2)
    stale_opp_o = across_cores(stale_opp_2)
    x_own_o = across_cores(x_own)
    student = contrib(places, h, NB, NB_O, nb_x, live_nb_o, student)
    t_near = contrib(places, h, NB, NB_O, stale_nb_2, stale_nb_o, t_near)

    far_3, came_3, nb_3 = after(
        (live_far_mid, came_a, stale_nb), x_own_o, student, t_near, stale_opp_o
    )
    stale_far = along_z(nb_3, MID)
    came_b = along_z(send_or_pass(places, h, far_3, fit, h.shape[1] // 2 // live.shape[1] - fit), PAIR)
    came_x, mid_x = after((came_3, live_mid), x_nb)
    live_opp = choose(places, END, came_x, mid_x)
    x_opp = near_over_x(live_opp, False)
    live_opp_o = across_cores(live_opp)
    x_nb_o = across_cores(x_nb)
    student = contrib(places, h, OPP, OPP_O, live_opp, live_opp_o, student)

    stale_far, came_4, far_4 = after((stale_far, came_b, far_3), x_opp, live_opp_o, student, x_nb_o)
    stale_far_o = across_cores(stale_far)
    t_mine, t_end = teachers(
        places, h, t_near, stale_opp, stale_opp_o, stale_far, stale_far_o, came_3, came_4
    )
    live_far = choose(places, END, came_4, far_4)
    x_far = near_over_x(live_far, False)
    live_far_o = across_cores(live_far)
    x_opp_o = across_cores(x_opp)
    student = contrib(places, h, FAR, FAR_O, live_far, live_far_o, student)

    target_1 = partner(t_mine, "mp", 0)
    route = []
    for m in range(2):
        for a, b in OUT:
            for core in range(2):
                route.append((8 * m + 2 * a + core, 8 * (1 - m) + 2 * b + core))
    target_2 = lax.ppermute(t_end, ("mp", "fsdp"), route)
    mismatch = difference(places, student, target_1, target_2, match)
    mismatch_o = partner(mismatch, "tp", 0)
    (x_far,) = after((x_far,), mismatch)
    x_far_o = across_cores(x_far)
    grad = gradient(
        places, mismatch, mismatch_o,
        (live, live_o, live_nb, live_nb_o), (live_opp, live_opp_o, live_far, live_far_o),
        (x_own, x_own_o, x_nb, x_nb_o), (x_opp, x_opp_o, x_far, x_far_o),
    )
    return grad[None]


def solution(mesh):
    in_specs = (
        P("mp", "fsdp", None),
        P("mp", "fsdp", "tp"),
        P("mp", "fsdp", "tp"),
        P("mp", "fsdp"),
    )
    out_specs = P("mp", "fsdp", "tp")
    line = mesh.shape["fsdp"] == 8 and mesh.shape["tp"] == 2 and mesh.shape["mp"] == 2
    body = line_of_four if line else general
    return jax.shard_map(body, mesh=mesh, in_specs=in_specs, out_specs=out_specs, check_vma=False)
```

```python
import jax
import jax.numpy as jnp
import numpy as np
from jax import lax
from jax.experimental import pallas as pl
from jax.experimental.pallas import tpu as pltpu
from jax.sharding import PartitionSpec as P

PAIR = ((0, 1), (1, 0), (2, 3), (3, 2))
MID = ((1, 2), (2, 1))
OUT = ((1, 0), (2, 3))

OWN, OWN_O, NB, NB_O, OPP, OPP_O, FAR, FAR_O, END, NEAR, HALF, PIECE = range(12)


def table():
    rows = []
    for f in range(8):
        for x in range(2):
            z, c = f // 2, f % 2
            half = z // 2
            opp, far = (2, 3) if half == 0 else (1, 0)
            near = int(half == x)
            first = z % 2 if near else half
            row = []
            for q in (z, z ^ 1, opp, far):
                row += [2 * q + c, 2 * q + 1 - c]
            row += [int(z in (0, 3)), near, 1 - half]
            for q in (first, 1 - first):
                row += [2 * q + c, 2 * q + 1 - c]
            rows.append(row)
    return np.array(rows, np.int32)


def partner(block, axis, apart):
    count = lax.axis_size(axis)
    route = []
    for low in range(count):
        high = low | 1 << apart
        if high != low and high < count:
            route += [(low, high), (high, low)]
    return lax.ppermute(block, axis, route)


def along_z(block, pairs):
    route = [(2 * a + c, 2 * b + c) for a, b in pairs for c in range(2)]
    return lax.ppermute(block, "fsdp", route)


def across_cores(block):
    return partner(block, "fsdp", 0)


def over_x(block, middle):
    route = []
    for f in range(8):
        half, z = f // 4, f // 2
        if middle in (False, True):
            route.append((2 * f + 1 - half, 2 * f + half))
        if middle is None or z in ((1, 2) if middle is True else (0, 3) if middle == END else ()):
            route.append((2 * f + half, 2 * f + 1 - half))
    return lax.ppermute(block, ("fsdp", "tp"), route)


def after(values, *gates):
    out = lax.optimization_barrier((tuple(values), gates))
    return out[0]


def dot(a, b):
    return jnp.dot(a, b, preferred_element_type=jnp.float32)


def dot_t(a, b):
    return lax.dot_general(a, b, (((1,), (1,)), ((), ())), preferred_element_type=jnp.float32)


def call(body, places, operands, outs, name):
    single = not isinstance(outs, (list, tuple))
    shapes = [outs] if single else list(outs)
    out = pl.pallas_call(
        body,
        out_shape=shapes,
        in_specs=[pl.BlockSpec(memory_space=pltpu.SMEM)] + [pl.BlockSpec(memory_space=pltpu.VMEM)] * len(operands),
        out_specs=[pl.BlockSpec(memory_space=pltpu.VMEM)] * len(shapes),
        cost_estimate=pl.CostEstimate(flops=1, bytes_accessed=1, transcendentals=0),
        compiler_params=pltpu.CompilerParams(vmem_limit_bytes=16 * 2 ** 20),
        name=name,
    )(places, *operands)
    return out[0] if single else out


def columns(ref, start, size):
    return ref[:, pl.ds(pl.multiple_of(start, 128), size)]


def contrib(places, h, mine, other, weight, weight_o, total=None):
    tokens, rows, cols = h.shape[0], *weight.shape

    def body(s, h_ref, w, wo, *rest):
        value = dot(columns(h_ref, s[mine] * rows, rows), w[...])
        value = value + dot(columns(h_ref, s[other] * rows, rows), wo[...])
        if total is not None:
            value = value + rest[0][...]
        rest[-1][...] = value

    operands = [h, weight, weight_o] + ([] if total is None else [total])
    return call(body, places, operands, jax.ShapeDtypeStruct((tokens, cols), jnp.float32), "contrib")


def as_rows(places, h, shape, first, piece=None):
    tokens, (rows, cols) = h.shape[0], shape
    total = h.shape[1] // 2

    def body(s, h_ref, *refs):
        out = refs[-1]

        @pl.when(s[END] == 1)
        def _():
            count = min(rows // tokens, total // cols - first)
            for k in range(count):
                start = s[HALF] * total + (first + k) * cols
                out[k * tokens:(k + 1) * tokens, :] = columns(h_ref, start, cols)
            if count * tokens < rows:
                out[count * tokens:, :] = jnp.zeros((rows - count * tokens, cols), out.dtype)

        @pl.when(s[END] == 0)
        def _():
            out[...] = jnp.zeros(shape, out.dtype) if piece is None else refs[0][...]

    return call(
        body, places, [h] + ([] if piece is None else [piece]), jax.ShapeDtypeStruct(shape, h.dtype), "as_rows"
    )


def choose(places, flag, yes, no):
    def body(s, yes_ref, no_ref, out):
        @pl.when(s[flag] == 1)
        def _():
            out[...] = yes_ref[...]

        @pl.when(s[flag] == 0)
        def _():
            out[...] = no_ref[...]

    return call(body, places, [yes, no], jax.ShapeDtypeStruct(yes.shape, yes.dtype), "choose")


def tick(places, value):
    def body(s, value_ref, out):
        out[...] = value_ref[:16, :128]

    return call(body, places, [value], jax.ShapeDtypeStruct((16, 128), value.dtype), "tick")


def to_opposite(places, h, total, nb, nb_o, opp, opp_o):
    tokens, (rows, cols) = h.shape[0], nb.shape

    def body(s, h_ref, total_ref, n, no, p, po, out):
        value = total_ref[...]
        for place, weight in ((NB, n), (NB_O, no)):
            value = value + dot(columns(h_ref, s[place] * rows, rows), weight[...])
        out[...] = value

        @pl.when(s[END] == 0)
        def _():
            more = dot(columns(h_ref, s[OPP] * rows, rows), p[...])
            out[...] += more + dot(columns(h_ref, s[OPP_O] * rows, rows), po[...])

    return call(
        body, places, [h, total, nb, nb_o, opp, opp_o], jax.ShapeDtypeStruct((tokens, cols), jnp.float32), "to_opposite"
    )


def teachers(places, h, t_near, stale_opp, stale_opp_o, stale_far, stale_far_o, came_a, came_b):
    tokens, (rows, cols) = h.shape[0], stale_opp.shape
    fit = rows // tokens
    width = h.shape[1] // 2

    def body(s, h_ref, near, w, wo, v, vo, ca, cb, mine, sent, held):
        @pl.when(s[END] == 1)
        def _():
            mine[...] = near[...].astype(mine.dtype)
            sent[...] = jnp.zeros(sent.shape, sent.dtype)

        @pl.when(s[END] == 0)
        def _():
            for k in range(width // cols):
                source, j = (ca, k) if k < fit else (cb, k - fit)
                held[:, k * cols:(k + 1) * cols] = source[j * tokens:(j + 1) * tokens, :]

            def away(place):
                return columns(held, s[place] * rows - s[HALF] * width, rows)

            end = dot(away(OPP), w[...]) + dot(away(OPP_O), wo[...])
            both = jnp.concatenate([columns(h_ref, s[FAR] * rows, rows), away(FAR)], axis=0)
            both_o = jnp.concatenate([columns(h_ref, s[FAR_O] * rows, rows), away(FAR_O)], axis=0)
            far = dot(both, v[...]) + dot(both_o, vo[...])
            mine[...] = (near[...] + far[:tokens]).astype(mine.dtype)
            sent[...] = (end + far[tokens:]).astype(sent.dtype)

    operands = [h, t_near, stale_opp, stale_opp_o, stale_far, stale_far_o, came_a, came_b]
    out = jax.ShapeDtypeStruct((tokens, cols), jnp.bfloat16)

    def with_scratch(*refs):
        pl.run_scoped(lambda held: body(*refs, held), pltpu.VMEM((tokens, width), h.dtype))

    return call(with_scratch, places, operands, [out, out], "teachers")


def difference(places, student, target_1, target_2, match):
    tokens = student.shape[0]

    def body(s, student_ref, one, two, match_ref, out):
        teacher = (one[...].astype(jnp.float32) + two[...].astype(jnp.float32)).astype(jnp.bfloat16)
        rows = lax.broadcasted_iota(jnp.int32, (tokens, tokens), 0)
        pick = (match_ref[...] == rows).astype(jnp.bfloat16)
        target = lax.dot_general(
            pick, teacher, (((0,), (0,)), ((), ())), preferred_element_type=jnp.float32
        )
        out[...] = (student_ref[...] - target).astype(out.dtype)

    operands = [student, target_1, target_2, match]
    return call(body, places, operands, jax.ShapeDtypeStruct(student.shape, jnp.bfloat16), "difference")


def gradient(places, left, choices, total=None):
    tokens = left.shape[0]
    rows, cols = choices[0][0].shape
    pieces = []
    for choice in choices:
        pieces += [p for p in choice if not any(p is q for q in pieces)]
    where = [[next(j for j, q in enumerate(pieces) if q is p) for p in choice] for choice in choices]
    dtype = jnp.float32 if total is None else left.dtype

    def body(s, left_ref, *refs):
        out = refs[-1]

        def run(choice):
            for k in range(4):
                start = pl.multiple_of(s[PIECE + k] * rows, 128)
                value = dot_t(left_ref[...], refs[where[choice][k]][...])
                if total is not None:
                    value = value + refs[len(pieces)][:, pl.ds(start, rows)]
                out[:, pl.ds(start, rows)] = value.astype(out.dtype)

        if where[0] == where[1]:
            pl.when(s[NEAR] == 0)(lambda: run(0))
        else:
            pl.when((s[NEAR] == 0) & (s[END] == 0))(lambda: run(0))
            pl.when((s[NEAR] == 0) & (s[END] == 1))(lambda: run(1))
        pl.when(s[NEAR] == 1)(lambda: run(2))

    operands = [left, *pieces] + ([] if total is None else [total])
    return call(body, places, operands, jax.ShapeDtypeStruct((tokens, 4 * rows), dtype), "gradient")


def general(hidden, live_weight, stale_weight, match):
    hidden_rows = hidden[0]
    live_full = lax.all_gather(live_weight[0], "fsdp", axis=0, tiled=True)
    student = dot(hidden_rows, live_full)
    stale_full = lax.all_gather(stale_weight[0], "fsdp", axis=0, tiled=True)
    teacher = dot(hidden_rows, stale_full).astype(jnp.bfloat16)
    teacher = partner(teacher, "mp", 0)
    target = jnp.take(teacher, match[0], axis=0)
    mismatch = (student - target.astype(jnp.float32)).astype(jnp.bfloat16)
    partial_value = dot_t(mismatch, live_full).astype(jnp.bfloat16)
    summed = lax.psum_scatter(partial_value, "tp", scatter_dimension=1, tiled=True)
    return summed[None]


def line_of_four(hidden, live_weight, stale_weight, match):
    h, live, stale = hidden[0], live_weight[0], stale_weight[0]
    fit = live.shape[0] // h.shape[0]
    place = 2 * lax.axis_index("fsdp") + lax.axis_index("tp")
    places = lax.dynamic_index_in_dim(jnp.asarray(table()), place, 0, keepdims=False)

    live_mid = along_z(live, MID)
    live_nb = along_z(live, PAIR)
    stale_opp = along_z(stale, MID)
    stale_nb = along_z(stale, PAIR)
    x_1 = over_x(live, False)
    live_o = across_cores(live)
    stale_o = across_cores(stale)
    student = contrib(places, h, OWN, OWN_O, live, live_o)
    t_near = contrib(places, h, OWN, OWN_O, stale, stale_o)

    mid_2, nb_2, s_opp, s_nb = after(
        (live_mid, live_nb, stale_opp, stale_nb), tick(places, stale_nb), student, t_near
    )
    live_far_mid = along_z(nb_2, MID)
    came_a = along_z(as_rows(places, h, live.shape, 0, mid_2), PAIR)
    nb_x, mid_x, own_x, s_opp, s_nb = after((nb_2, mid_2, x_1, s_opp, s_nb), live_o, stale_o)
    x_2 = over_x(choose(places, NEAR, mid_x, nb_x), True)
    live_nb_o = across_cores(nb_x)
    stale_nb_o = across_cores(s_nb)
    stale_opp_o = across_cores(s_opp)
    x_1_o = across_cores(own_x)
    student = contrib(places, h, NB, NB_O, nb_x, live_nb_o, student)
    t_near = to_opposite(places, h, t_near, s_nb, stale_nb_o, s_opp, stale_opp_o)

    far_3, came_3, nb_3 = after((live_far_mid, came_a, stale_nb), tick(places, came_a), student, t_near)
    stale_far = along_z(nb_3, MID)
    came_b = along_z(as_rows(places, h, live.shape, fit, far_3), PAIR)
    came_x, far_x, x_2 = after((came_3, far_3, x_2), x_1_o, student, t_near)
    x_3 = over_x(choose(places, END, came_x, far_x), None)

    stale_far, came_4 = after((stale_far, came_b), tick(places, came_b))
    stale_far_o = across_cores(stale_far)
    x_4 = over_x(came_4, END)
    (t_near,) = after((t_near,), x_3)
    t_mine, t_end = teachers(
        places, h, t_near, stale_opp, stale_opp_o, stale_far, stale_far_o, came_3, came_4
    )
    came_t, mid_t, far_t, came_t4, x_2t, x_3t = after((came_3, live_mid, far_3, came_4, x_2, x_3), t_mine)
    live_opp = choose(places, END, came_t, mid_t)
    live_far = choose(places, END, came_t4, far_t)
    live_opp_o = across_cores(live_opp)
    live_far_o = across_cores(live_far)
    x_2_o = across_cores(x_2t)
    x_3_o = across_cores(x_3t)
    student = contrib(places, h, OPP, OPP_O, live_opp, live_opp_o, student)
    student = contrib(places, h, FAR, FAR_O, live_far, live_far_o, student)

    target_1 = partner(t_mine, "mp", 0)
    route = []
    for m in range(2):
        for a, b in OUT:
            for core in range(2):
                route.append((8 * m + 2 * a + core, 8 * (1 - m) + 2 * b + core))
    target_2 = lax.ppermute(t_end, ("mp", "fsdp"), route)
    mismatch = difference(places, student, target_1, target_2, match)
    mismatch_o = partner(mismatch, "tp", 0)
    (x_4,) = after((x_4,), mismatch)
    x_4_o = across_cores(x_4)
    own = gradient(
        places, mismatch,
        ((live_opp, live_opp_o, live_far, live_far_o),) * 2 + ((live, live_o, live_nb, live_nb_o),),
    )
    grad = gradient(
        places, mismatch_o,
        ((x_2, x_2_o, x_3, x_3_o), (x_3, x_3_o, x_4, x_4_o), (x_1, x_1_o, x_2, x_2_o)), own,
    )
    return grad[None]


def solution(mesh):
    in_specs = (
        P("mp", "fsdp", None),
        P("mp", "fsdp", "tp"),
        P("mp", "fsdp", "tp"),
        P("mp", "fsdp"),
    )
    out_specs = P("mp", "fsdp", "tp")
    line = mesh.shape["fsdp"] == 8 and mesh.shape["tp"] == 2 and mesh.shape["mp"] == 2
    body = line_of_four if line else general
    return jax.shard_map(body, mesh=mesh, in_specs=in_specs, out_specs=out_specs, check_vma=False)
```

```python
import jax
import jax.numpy as jnp
import numpy as np
from jax import lax
from jax.experimental import pallas as pl
from jax.experimental.pallas import tpu as pltpu
from jax.sharding import PartitionSpec as P

PAIR = ((0, 1), (1, 0), (2, 3), (3, 2))
MID = ((1, 2), (2, 1))
IN = ((0, 1), (3, 2))
OUT = ((1, 0), (2, 3))

OWN, OWN_O, NB, NB_O, OPP, OPP_O, FAR, FAR_O, END, NEAR, SENT, CAME, PIECE = range(13)


def table():
    rows = []
    for f in range(8):
        for x in range(2):
            z, c = f // 2, f % 2
            half = z // 2
            opp, far = (2, 3) if half == 0 else (1, 0)
            near = int(half == x)
            first = z % 2 if near else half
            row = []
            for q in (z, z ^ 1, opp, far):
                row += [2 * q + c, 2 * q + 1 - c]
            row += [int(z in (0, 3)), near, int(z == 0), int(z == 1)]
            for q in (first, 1 - first):
                row += [2 * q + c, 2 * q + 1 - c]
            rows.append(row)
    return np.array(rows, np.int32)


def partner(block, axis, apart):
    count = lax.axis_size(axis)
    route = []
    for low in range(count):
        high = low | 1 << apart
        if high != low and high < count:
            route += [(low, high), (high, low)]
    return lax.ppermute(block, axis, route)


def along_z(block, pairs):
    route = [(2 * a + c, 2 * b + c) for a, b in pairs for c in range(2)]
    return lax.ppermute(block, "fsdp", route)


def across_cores(block):
    return partner(block, "fsdp", 0)


def over_x(block, middle):
    route = []
    for f in range(8):
        half, z = f // 4, f // 2
        if middle in (False, True):
            route.append((2 * f + 1 - half, 2 * f + half))
        if middle is None or z in ((1, 2) if middle is True else (0, 3) if middle == END else ()):
            route.append((2 * f + half, 2 * f + 1 - half))
    return lax.ppermute(block, ("fsdp", "tp"), route)


def after(values, *gates):
    out = lax.optimization_barrier((tuple(values), gates))
    return out[0]


def dot(a, b):
    return jnp.dot(a, b, preferred_element_type=jnp.float32)


def dot_t(a, b):
    return lax.dot_general(a, b, (((1,), (1,)), ((), ())), preferred_element_type=jnp.float32)


def call(body, places, operands, outs, name):
    single = not isinstance(outs, (list, tuple))
    shapes = [outs] if single else list(outs)
    out = pl.pallas_call(
        body,
        out_shape=shapes,
        in_specs=[pl.BlockSpec(memory_space=pltpu.SMEM)] + [pl.BlockSpec(memory_space=pltpu.VMEM)] * len(operands),
        out_specs=[pl.BlockSpec(memory_space=pltpu.VMEM)] * len(shapes),
        cost_estimate=pl.CostEstimate(flops=1, bytes_accessed=1, transcendentals=0),
        compiler_params=pltpu.CompilerParams(vmem_limit_bytes=16 * 2 ** 20),
        name=name,
    )(places, *operands)
    return out[0] if single else out


def columns(ref, start, size):
    return ref[:, pl.ds(pl.multiple_of(start, 128), size)]


def contrib(places, h, mine, other, pairs, total=None):
    tokens, (rows, cols) = h.shape[0], pairs[0][0].shape

    def body(s, h_ref, *refs):
        def run(w, wo):
            value = dot(columns(h_ref, s[mine] * rows, rows), w[...])
            value = value + dot(columns(h_ref, s[other] * rows, rows), wo[...])
            if total is not None:
                value = value + refs[-2][...]
            refs[-1][...] = value

        if len(pairs) == 1:
            run(*refs[:2])
        else:
            for end in (0, 1):
                pl.when(s[END] == end)(lambda end=end: run(*refs[2 * end:2 * end + 2]))

    operands = [h] + [p for pair in pairs for p in pair] + ([] if total is None else [total])
    return call(body, places, operands, jax.ShapeDtypeStruct((tokens, cols), jnp.float32), "contrib")


def as_rows(places, h, shape, first, piece=None):
    tokens, (rows, cols) = h.shape[0], shape
    quarter = h.shape[1] // 4
    total = 3 * quarter

    def body(s, h_ref, *refs):
        out = refs[-1]

        @pl.when(s[END] == 1)
        def _():
            for k in range(rows // tokens):
                start = (first + k) * cols
                size = min(cols, total - start)
                out[k * tokens:(k + 1) * tokens, :size] = columns(h_ref, s[SENT] * quarter + start, size)
                if size < cols:
                    out[k * tokens:(k + 1) * tokens, size:] = jnp.zeros((tokens, cols - size), out.dtype)

        @pl.when(s[END] == 0)
        def _():
            out[...] = jnp.zeros(shape, out.dtype) if piece is None else refs[0][...]

    return call(
        body, places, [h] + ([] if piece is None else [piece]), jax.ShapeDtypeStruct(shape, h.dtype), "as_rows"
    )


def choose(places, flag, yes, no):
    def body(s, yes_ref, no_ref, out):
        @pl.when(s[flag] == 1)
        def _():
            out[...] = yes_ref[...]

        @pl.when(s[flag] == 0)
        def _():
            out[...] = no_ref[...]

    return call(body, places, [yes, no], jax.ShapeDtypeStruct(yes.shape, yes.dtype), "choose")


def tick(places, value):
    def body(s, value_ref, out):
        out[...] = value_ref[:16, :128]

    return call(body, places, [value], jax.ShapeDtypeStruct((16, 128), value.dtype), "tick")


def near_ends(places, h, total, nb, nb_o, opp, opp_o):
    tokens, (rows, cols) = h.shape[0], nb.shape

    def body(s, h_ref, total_ref, n, no, p, po, out):
        @pl.when(s[END] == 1)
        def _():
            out[...] = total_ref[...]

        @pl.when(s[END] == 0)
        def _():
            value = total_ref[...]
            for place, weight in ((NB, n), (NB_O, no), (OPP, p), (OPP_O, po)):
                value = value + dot(columns(h_ref, s[place] * rows, rows), weight[...])
            out[...] = value

    return call(
        body, places, [h, total, nb, nb_o, opp, opp_o], jax.ShapeDtypeStruct((tokens, cols), jnp.float32), "near_ends"
    )


def teachers(places, h, t_near, weights, came):
    tokens, (rows, cols) = h.shape[0], weights[0].shape
    quarter = h.shape[1] // 4

    def body(s, h_ref, near, w, wo, p, po, v, vo, ca, cb, mine, sent, held):
        @pl.when(s[END] == 1)
        def _():
            mine[...] = near[...].astype(mine.dtype)
            sent[...] = jnp.zeros(sent.shape, sent.dtype)

        @pl.when(s[END] == 0)
        def _():
            for k in range(-(-3 * quarter // cols)):
                source, j = (ca, k) if k < rows // tokens else (cb, k - rows // tokens)
                size = min(cols, 3 * quarter - k * cols)
                held[:, k * cols:k * cols + size] = source[j * tokens:(j + 1) * tokens, :size]

            def away(place):
                return columns(held, s[place] * rows - s[CAME] * quarter, rows)

            end = dot(away(OWN), w[...]) + dot(away(OWN_O), wo[...])
            end = end + dot(away(OPP), p[...]) + dot(away(OPP_O), po[...])
            own = jnp.concatenate([columns(h_ref, s[FAR] * rows, rows), away(FAR)], axis=0)
            own_o = jnp.concatenate([columns(h_ref, s[FAR_O] * rows, rows), away(FAR_O)], axis=0)
            far = dot(own, v[...]) + dot(own_o, vo[...])
            mine[...] = (near[...] + far[:tokens]).astype(mine.dtype)
            sent[...] = (end + far[tokens:]).astype(sent.dtype)

    out = jax.ShapeDtypeStruct((tokens, cols), jnp.bfloat16)

    def with_scratch(*refs):
        pl.run_scoped(lambda held: body(*refs, held), pltpu.VMEM((tokens, 3 * quarter), h.dtype))

    return call(with_scratch, places, [h, t_near, *weights, *came], [out, out], "teachers")


def difference(places, student, target_1, target_2, match):
    tokens = student.shape[0]

    def body(s, student_ref, one, two, match_ref, out):
        teacher = (one[...].astype(jnp.float32) + two[...].astype(jnp.float32)).astype(jnp.bfloat16)
        rows = lax.broadcasted_iota(jnp.int32, (tokens, tokens), 0)
        pick = (match_ref[...] == rows).astype(jnp.bfloat16)
        target = lax.dot_general(
            pick, teacher, (((0,), (0,)), ((), ())), preferred_element_type=jnp.float32
        )
        out[...] = (student_ref[...] - target).astype(out.dtype)

    operands = [student, target_1, target_2, match]
    return call(body, places, operands, jax.ShapeDtypeStruct(student.shape, jnp.bfloat16), "difference")


def gradient(places, left, choices, total=None):
    tokens = left.shape[0]
    rows, cols = choices[0][0].shape
    pieces = []
    for choice in choices:
        pieces += [p for p in choice if not any(p is q for q in pieces)]
    where = [[next(j for j, q in enumerate(pieces) if q is p) for p in choice] for choice in choices]
    dtype = jnp.float32 if total is None else left.dtype

    def body(s, left_ref, *refs):
        out = refs[-1]

        def run(choice):
            for k in range(4):
                start = pl.multiple_of(s[PIECE + k] * rows, 128)
                value = dot_t(left_ref[...], refs[where[choice][k]][...])
                if total is not None:
                    value = value + refs[len(pieces)][:, pl.ds(start, rows)]
                out[:, pl.ds(start, rows)] = value.astype(out.dtype)

        if where[0] == where[1]:
            pl.when(s[NEAR] == 0)(lambda: run(0))
        else:
            pl.when((s[NEAR] == 0) & (s[END] == 0))(lambda: run(0))
            pl.when((s[NEAR] == 0) & (s[END] == 1))(lambda: run(1))
        pl.when(s[NEAR] == 1)(lambda: run(2))

    operands = [left, *pieces] + ([] if total is None else [total])
    return call(body, places, operands, jax.ShapeDtypeStruct((tokens, 4 * rows), dtype), "gradient")


def general(hidden, live_weight, stale_weight, match):
    hidden_rows = hidden[0]
    live_full = lax.all_gather(live_weight[0], "fsdp", axis=0, tiled=True)
    student = dot(hidden_rows, live_full)
    stale_full = lax.all_gather(stale_weight[0], "fsdp", axis=0, tiled=True)
    teacher = dot(hidden_rows, stale_full).astype(jnp.bfloat16)
    teacher = partner(teacher, "mp", 0)
    target = jnp.take(teacher, match[0], axis=0)
    mismatch = (student - target.astype(jnp.float32)).astype(jnp.bfloat16)
    partial_value = dot_t(mismatch, live_full).astype(jnp.bfloat16)
    summed = lax.psum_scatter(partial_value, "tp", scatter_dimension=1, tiled=True)
    return summed[None]


def line_of_four(hidden, live_weight, stale_weight, match):
    h, live, stale = hidden[0], live_weight[0], stale_weight[0]
    fit = live.shape[0] // h.shape[0]
    place = 2 * lax.axis_index("fsdp") + lax.axis_index("tp")
    places = lax.dynamic_index_in_dim(jnp.asarray(table()), place, 0, keepdims=False)

    live_mid = along_z(live, MID)
    live_nb = along_z(live, PAIR)
    x_1 = over_x(live, False)
    live_o = across_cores(live)
    stale_o = across_cores(stale)
    student = contrib(places, h, OWN, OWN_O, [(live, live_o)])
    t_near = contrib(places, h, OWN, OWN_O, [(stale, stale_o)])

    mid_2, nb_2 = after((live_mid, live_nb), tick(places, live_nb), student, t_near)
    live_far_mid = along_z(nb_2, MID)
    both = along_z(choose(places, END, stale, mid_2), PAIR)
    nb_x, mid_x, own_x = after((nb_2, mid_2, x_1), live_o, stale_o)
    x_2 = over_x(choose(places, NEAR, mid_x, nb_x), True)
    live_nb_o = across_cores(nb_x)
    live_mid_o = across_cores(mid_x)
    x_1_o = across_cores(own_x)

    far_3, both_3, stale_3 = after((live_far_mid, both, stale), tick(places, both))
    stale_opp = along_z(stale_3, MID)
    came_a = along_z(as_rows(places, h, live.shape, 0, far_3), PAIR)
    both_x, far_x, x_2, nb_x3 = after((both_3, far_3, x_2, live_nb), live_nb_o, live_mid_o, x_1_o)
    x_3 = over_x(choose(places, END, both_x, far_x), None)
    both_o = across_cores(both_3)
    far_3o = across_cores(far_3)
    student = contrib(places, h, NB, NB_O, [(nb_x3, live_nb_o)], student)

    both_4, opp_4, came_4 = after((both_3, stale_opp, came_a), tick(places, came_a), student)
    rest = -(-3 * h.shape[1] // (4 * live.shape[1])) - fit
    (h_4,) = after((h,), stale_3)
    more = as_rows(places, h_4, (rest * h.shape[0], live.shape[1]), fit)
    (more,) = after((more,), opp_4)
    stale_far = along_z(both_4, MID)
    came_b = along_z(more, IN)
    came_x, x_3, opp_x = after((came_4, x_3, opp_4), both_o, far_3o)
    x_4 = over_x(came_x, END)
    stale_opp_o = across_cores(opp_4)
    came_4o = across_cores(came_4)
    student = contrib(places, h, OPP, OPP_O, [(live_mid, live_mid_o), (both_3, both_o)], student)
    t_near = near_ends(places, h, t_near, both_4, both_o, opp_4, stale_opp_o)

    stale_far, came_b = after((stale_far, came_b), tick(places, came_b), student, t_near)
    stale_far_o = across_cores(stale_far)
    (t_near,) = after((t_near,), x_4, came_4o)
    t_mine, t_end = teachers(
        places, h, t_near, (stale, stale_o, opp_4, stale_opp_o, stale_far, stale_far_o), (came_4, came_b)
    )
    x_2t, x_3t, x_4t, student = after((x_2, x_3, x_4, student), t_mine)
    x_2_o = across_cores(x_2t)
    x_3_o = across_cores(x_3t)
    x_4_o = across_cores(x_4t)
    student = contrib(places, h, FAR, FAR_O, [(far_3, far_3o), (came_4, came_4o)], student)

    target_1 = partner(t_mine, "mp", 0)
    route = []
    for m in range(2):
        for a, b in OUT:
            for core in range(2):
                route.append((8 * m + 2 * a + core, 8 * (1 - m) + 2 * b + core))
    target_2 = lax.ppermute(t_end, ("mp", "fsdp"), route)
    mismatch = difference(places, student, target_1, target_2, match)
    mismatch_o = partner(mismatch, "tp", 0)
    own = gradient(
        places, mismatch,
        (
            (live_mid, live_mid_o, far_3, far_3o),
            (both_3, both_o, came_4, came_4o),
            (live, live_o, live_nb, live_nb_o),
        ),
    )
    grad = gradient(
        places, mismatch_o,
        ((x_2, x_2_o, x_3, x_3_o), (x_3, x_3_o, x_4, x_4_o), (x_1, x_1_o, x_2, x_2_o)), own,
    )
    return grad[None]


def solution(mesh):
    in_specs = (
        P("mp", "fsdp", None),
        P("mp", "fsdp", "tp"),
        P("mp", "fsdp", "tp"),
        P("mp", "fsdp"),
    )
    out_specs = P("mp", "fsdp", "tp")
    line = mesh.shape["fsdp"] == 8 and mesh.shape["tp"] == 2 and mesh.shape["mp"] == 2
    body = line_of_four if line else general
    return jax.shard_map(body, mesh=mesh, in_specs=in_specs, out_specs=out_specs, check_vma=False)
```

```python
import jax
import jax.numpy as jnp
import numpy as np
from jax import lax
from jax.experimental import pallas as pl
from jax.experimental.pallas import tpu as pltpu
from jax.sharding import PartitionSpec as P

PAIR = ((0, 1), (1, 0), (2, 3), (3, 2))
MID = ((1, 2), (2, 1))
IN = ((0, 1), (3, 2))
OUT = ((1, 0), (2, 3))

OWN, OWN_O, NB, NB_O, OPP, OPP_O, FAR, FAR_O, END, NEAR, SENT, CAME, PIECE = range(13)


def table():
    rows = []
    for f in range(8):
        for x in range(2):
            z, c = f // 2, f % 2
            half = z // 2
            opp, far = (2, 3) if half == 0 else (1, 0)
            near = int(half == x)
            first = z % 2 if near else half
            row = []
            for q in (z, z ^ 1, opp, far):
                row += [2 * q + c, 2 * q + 1 - c]
            row += [int(z in (0, 3)), near, int(z == 0), int(z == 1)]
            for q in (first, 1 - first):
                row += [2 * q + c, 2 * q + 1 - c]
            rows.append(row)
    return np.array(rows, np.int32)


def partner(block, axis, apart):
    count = lax.axis_size(axis)
    route = []
    for low in range(count):
        high = low | 1 << apart
        if high != low and high < count:
            route += [(low, high), (high, low)]
    return lax.ppermute(block, axis, route)


def along_z(block, pairs):
    route = [(2 * a + c, 2 * b + c) for a, b in pairs for c in range(2)]
    return lax.ppermute(block, "fsdp", route)


def across_cores(block):
    return partner(block, "fsdp", 0)


def over_x(block, middle):
    route = []
    for f in range(8):
        half, z = f // 4, f // 2
        if middle in (False, True):
            route.append((2 * f + 1 - half, 2 * f + half))
        if middle is None or z in ((1, 2) if middle is True else (0, 3) if middle == END else ()):
            route.append((2 * f + half, 2 * f + 1 - half))
    return lax.ppermute(block, ("fsdp", "tp"), route)


def after(values, *gates):
    out = lax.optimization_barrier((tuple(values), gates))
    return out[0]


def dot(a, b):
    return jnp.dot(a, b, preferred_element_type=jnp.float32)


def dot_t(a, b):
    return lax.dot_general(a, b, (((1,), (1,)), ((), ())), preferred_element_type=jnp.float32)


def call(body, places, operands, outs, name):
    single = not isinstance(outs, (list, tuple))
    shapes = [outs] if single else list(outs)
    out = pl.pallas_call(
        body,
        out_shape=shapes,
        in_specs=[pl.BlockSpec(memory_space=pltpu.SMEM)] + [pl.BlockSpec(memory_space=pltpu.VMEM)] * len(operands),
        out_specs=[pl.BlockSpec(memory_space=pltpu.VMEM)] * len(shapes),
        cost_estimate=pl.CostEstimate(flops=1, bytes_accessed=1, transcendentals=0),
        compiler_params=pltpu.CompilerParams(vmem_limit_bytes=16 * 2 ** 20),
        name=name,
    )(places, *operands)
    return out[0] if single else out


def columns(ref, start, size):
    return ref[:, pl.ds(pl.multiple_of(start, 128), size)]


def contrib(places, h, mine, other, pairs, total=None):
    tokens, (rows, cols) = h.shape[0], pairs[0][0].shape

    def body(s, h_ref, *refs):
        def run(w, wo):
            value = dot(columns(h_ref, s[mine] * rows, rows), w[...])
            value = value + dot(columns(h_ref, s[other] * rows, rows), wo[...])
            if total is not None:
                value = value + refs[-2][...]
            refs[-1][...] = value

        if len(pairs) == 1:
            run(*refs[:2])
        else:
            for end in (0, 1):
                pl.when(s[END] == end)(lambda end=end: run(*refs[2 * end:2 * end + 2]))

    operands = [h] + [p for pair in pairs for p in pair] + ([] if total is None else [total])
    return call(body, places, operands, jax.ShapeDtypeStruct((tokens, cols), jnp.float32), "contrib")


def as_rows(places, h, shape, first, piece=None):
    tokens, (rows, cols) = h.shape[0], shape
    quarter = h.shape[1] // 4
    total = 3 * quarter

    def body(s, h_ref, *refs):
        out = refs[-1]

        @pl.when(s[END] == 1)
        def _():
            for k in range(rows // tokens):
                start = (first + k) * cols
                size = min(cols, total - start)
                out[k * tokens:(k + 1) * tokens, :size] = columns(h_ref, s[SENT] * quarter + start, size)
                if size < cols:
                    out[k * tokens:(k + 1) * tokens, size:] = jnp.zeros((tokens, cols - size), out.dtype)

        @pl.when(s[END] == 0)
        def _():
            out[...] = jnp.zeros(shape, out.dtype) if piece is None else refs[0][...]

    return call(
        body, places, [h] + ([] if piece is None else [piece]), jax.ShapeDtypeStruct(shape, h.dtype), "as_rows"
    )


def choose(places, flag, yes, no):
    def body(s, yes_ref, no_ref, out):
        @pl.when(s[flag] == 1)
        def _():
            out[...] = yes_ref[...]

        @pl.when(s[flag] == 0)
        def _():
            out[...] = no_ref[...]

    return call(body, places, [yes, no], jax.ShapeDtypeStruct(yes.shape, yes.dtype), "choose")


def tick(places, value):
    def body(s, value_ref, out):
        out[...] = value_ref[:16, :128]

    return call(body, places, [value], jax.ShapeDtypeStruct((16, 128), value.dtype), "tick")


def near_ends(places, h, total, nb, nb_o, opp, opp_o):
    tokens, (rows, cols) = h.shape[0], nb.shape

    def body(s, h_ref, total_ref, n, no, p, po, out):
        @pl.when(s[END] == 1)
        def _():
            out[...] = total_ref[...]

        @pl.when(s[END] == 0)
        def _():
            value = total_ref[...]
            for place, weight in ((NB, n), (NB_O, no), (OPP, p), (OPP_O, po)):
                value = value + dot(columns(h_ref, s[place] * rows, rows), weight[...])
            out[...] = value

    return call(
        body, places, [h, total, nb, nb_o, opp, opp_o], jax.ShapeDtypeStruct((tokens, cols), jnp.float32), "near_ends"
    )


def teachers(places, h, t_near, weights, came):
    tokens, (rows, cols) = h.shape[0], weights[0].shape
    quarter = h.shape[1] // 4

    def body(s, h_ref, near, w, wo, p, po, v, vo, ca, cb, mine, sent, held):
        @pl.when(s[END] == 1)
        def _():
            mine[...] = near[...].astype(mine.dtype)
            sent[...] = jnp.zeros(sent.shape, sent.dtype)

        @pl.when(s[END] == 0)
        def _():
            for k in range(-(-3 * quarter // cols)):
                source, j = (ca, k) if k < rows // tokens else (cb, k - rows // tokens)
                size = min(cols, 3 * quarter - k * cols)
                held[:, k * cols:k * cols + size] = source[j * tokens:(j + 1) * tokens, :size]

            def away(place):
                return columns(held, s[place] * rows - s[CAME] * quarter, rows)

            end = dot(away(OWN), w[...]) + dot(away(OWN_O), wo[...])
            end = end + dot(away(OPP), p[...]) + dot(away(OPP_O), po[...])
            own = jnp.concatenate([columns(h_ref, s[FAR] * rows, rows), away(FAR)], axis=0)
            own_o = jnp.concatenate([columns(h_ref, s[FAR_O] * rows, rows), away(FAR_O)], axis=0)
            far = dot(own, v[...]) + dot(own_o, vo[...])
            mine[...] = (near[...] + far[:tokens]).astype(mine.dtype)
            sent[...] = (end + far[tokens:]).astype(sent.dtype)

    out = jax.ShapeDtypeStruct((tokens, cols), jnp.bfloat16)

    def with_scratch(*refs):
        pl.run_scoped(lambda held: body(*refs, held), pltpu.VMEM((tokens, 3 * quarter), h.dtype))

    return call(with_scratch, places, [h, t_near, *weights, *came], [out, out], "teachers")


def difference(places, student, target_1, target_2, match):
    tokens = student.shape[0]

    def body(s, student_ref, one, two, match_ref, out):
        teacher = (one[...].astype(jnp.float32) + two[...].astype(jnp.float32)).astype(jnp.bfloat16)
        rows = lax.broadcasted_iota(jnp.int32, (tokens, tokens), 0)
        pick = (match_ref[...] == rows).astype(jnp.bfloat16)
        target = lax.dot_general(
            pick, teacher, (((0,), (0,)), ((), ())), preferred_element_type=jnp.float32
        )
        out[...] = (student_ref[...] - target).astype(out.dtype)

    operands = [student, target_1, target_2, match]
    return call(body, places, operands, jax.ShapeDtypeStruct(student.shape, jnp.bfloat16), "difference")


def gradient(places, left, choices, total=None):
    tokens = left.shape[0]
    rows, cols = choices[0][0].shape
    pieces = []
    for choice in choices:
        pieces += [p for p in choice if not any(p is q for q in pieces)]
    where = [[next(j for j, q in enumerate(pieces) if q is p) for p in choice] for choice in choices]
    dtype = jnp.float32 if total is None else left.dtype

    def body(s, left_ref, *refs):
        out = refs[-1]

        def run(choice):
            for k in range(4):
                start = pl.multiple_of(s[PIECE + k] * rows, 128)
                value = dot_t(left_ref[...], refs[where[choice][k]][...])
                if total is not None:
                    value = value + refs[len(pieces)][:, pl.ds(start, rows)]
                out[:, pl.ds(start, rows)] = value.astype(out.dtype)

        if where[0] == where[1]:
            pl.when(s[NEAR] == 0)(lambda: run(0))
        else:
            pl.when((s[NEAR] == 0) & (s[END] == 0))(lambda: run(0))
            pl.when((s[NEAR] == 0) & (s[END] == 1))(lambda: run(1))
        pl.when(s[NEAR] == 1)(lambda: run(2))

    operands = [left, *pieces] + ([] if total is None else [total])
    return call(body, places, operands, jax.ShapeDtypeStruct((tokens, 4 * rows), dtype), "gradient")


def general(hidden, live_weight, stale_weight, match):
    hidden_rows = hidden[0]
    live_full = lax.all_gather(live_weight[0], "fsdp", axis=0, tiled=True)
    student = dot(hidden_rows, live_full)
    stale_full = lax.all_gather(stale_weight[0], "fsdp", axis=0, tiled=True)
    teacher = dot(hidden_rows, stale_full).astype(jnp.bfloat16)
    teacher = partner(teacher, "mp", 0)
    target = jnp.take(teacher, match[0], axis=0)
    mismatch = (student - target.astype(jnp.float32)).astype(jnp.bfloat16)
    partial_value = dot_t(mismatch, live_full).astype(jnp.bfloat16)
    summed = lax.psum_scatter(partial_value, "tp", scatter_dimension=1, tiled=True)
    return summed[None]


def line_of_four(hidden, live_weight, stale_weight, match):
    h, live, stale = hidden[0], live_weight[0], stale_weight[0]
    fit = live.shape[0] // h.shape[0]
    place = 2 * lax.axis_index("fsdp") + lax.axis_index("tp")
    places = lax.dynamic_index_in_dim(jnp.asarray(table()), place, 0, keepdims=False)

    live_mid = along_z(live, MID)
    live_nb = along_z(live, PAIR)
    x_1 = over_x(live, False)
    live_o = across_cores(live)
    stale_o = across_cores(stale)
    student = contrib(places, h, OWN, OWN_O, [(live, live_o)])
    t_near = contrib(places, h, OWN, OWN_O, [(stale, stale_o)])

    mid_2, nb_2 = after((live_mid, live_nb), tick(places, live_nb), student, t_near)
    live_far_mid = along_z(nb_2, MID)
    both = along_z(choose(places, END, stale, mid_2), PAIR)
    nb_x, mid_x, own_x = after((nb_2, mid_2, x_1), live_o, stale_o)
    x_2 = over_x(choose(places, NEAR, mid_x, nb_x), True)
    live_nb_o = across_cores(nb_x)
    live_mid_o = across_cores(mid_x)
    x_1_o = across_cores(own_x)

    far_3, both_3, stale_3 = after((live_far_mid, both, stale), tick(places, both))
    stale_opp = along_z(stale_3, MID)
    came_a = along_z(as_rows(places, h, live.shape, 0, far_3), PAIR)
    both_o = across_cores(both_3)
    both_x, far_x, x_2, nb_x3 = after((both_3, far_3, x_2, live_nb), live_nb_o, live_mid_o, x_1_o)
    x_3 = over_x(choose(places, END, both_x, far_x), None)
    far_3o = across_cores(far_3)
    student = contrib(places, h, NB, NB_O, [(nb_x3, live_nb_o)], student)

    both_4, opp_4, came_4 = after((both_3, stale_opp, came_a), tick(places, came_a), student)
    rest = -(-3 * h.shape[1] // (4 * live.shape[1])) - fit
    (h_4,) = after((h,), stale_3)
    more = as_rows(places, h_4, (rest * h.shape[0], live.shape[1]), fit)
    stale_opp_o = across_cores(opp_4)
    (more,) = after((more,), opp_4)
    stale_far = along_z(both_4, MID)
    came_b = along_z(more, IN)
    came_x, x_3 = after((came_4, x_3))
    x_4 = over_x(came_x, END)
    came_4o = across_cores(came_4)
    t_near = near_ends(places, h, t_near, both_4, both_o, opp_4, stale_opp_o)
    student = contrib(places, h, OPP, OPP_O, [(live_mid, live_mid_o), (both_3, both_o)], student)

    stale_far, came_b = after((stale_far, came_b), tick(places, came_b), student, t_near)
    stale_far_o = across_cores(stale_far)
    (t_near,) = after((t_near,), x_4, came_4o)
    t_mine, t_end = teachers(
        places, h, t_near, (stale, stale_o, opp_4, stale_opp_o, stale_far, stale_far_o), (came_4, came_b)
    )
    (student,) = after((student,), t_mine)
    x_2t, x_3t, x_4t = after((x_2, x_3, x_4), t_mine)
    student = contrib(places, h, FAR, FAR_O, [(far_3, far_3o), (came_4, came_4o)], student)
    x_2_o = across_cores(x_2t)
    x_3_o = across_cores(x_3t)
    x_4_o = across_cores(x_4t)

    target_1 = partner(t_mine, "mp", 0)
    route = []
    for m in range(2):
        for a, b in OUT:
            for core in range(2):
                route.append((8 * m + 2 * a + core, 8 * (1 - m) + 2 * b + core))
    target_2 = lax.ppermute(t_end, ("mp", "fsdp"), route)
    mismatch = difference(places, student, target_1, target_2, match)
    mismatch_o = partner(mismatch, "tp", 0)
    own = gradient(
        places, mismatch,
        (
            (live_mid, live_mid_o, far_3, far_3o),
            (both_3, both_o, came_4, came_4o),
            (live, live_o, live_nb, live_nb_o),
        ),
    )
    grad = gradient(
        places, mismatch_o,
        ((x_2, x_2_o, x_3, x_3_o), (x_3, x_3_o, x_4, x_4_o), (x_1, x_1_o, x_2, x_2_o)), own,
    )
    return grad[None]


def solution(mesh):
    in_specs = (
        P("mp", "fsdp", None),
        P("mp", "fsdp", "tp"),
        P("mp", "fsdp", "tp"),
        P("mp", "fsdp"),
    )
    out_specs = P("mp", "fsdp", "tp")
    line = mesh.shape["fsdp"] == 8 and mesh.shape["tp"] == 2 and mesh.shape["mp"] == 2
    body = line_of_four if line else general
    return jax.shard_map(body, mesh=mesh, in_specs=in_specs, out_specs=out_specs, check_vma=False)
```
